32 devices in a mesh: pts: 8 (over y, x, core), val: 4 (over z).
Axes of the slice: x: 2, y: 2, z: 4, core: 2. Of those that a mesh axis runs over, the one named last changes fastest.
Arguments:
- vectors: float32 [1, 512, 2048], P(None, 'val', 'pts'), may hold values from -6 to 6
- eval_energy: float32 [512], P('val'), may hold values from -2 to -0.2
- cond_energy: float32 [2048], P('pts'), may hold values from 0.2 to 2
- val_orbitals: float32 [512, 8192], P('pts', 'val'), may hold values from -0.25 to 0.25
- cond_orbitals: float32 [2048, 8192], P('val', 'pts'), may hold values from -0.125 to 0.125
- screened: float32 [8192, 8192], P('val', 'pts'), may hold values from -1.5 to 1.5
Outputs:
- filtered: float32 [1, 512, 2048], P(None, 'val', 'pts')
The draws below stay inside these ranges and needn't reach their ends.
All inputs are finite; a program needn't handle non-finite values.
Results may differ from the reference program's by a relative error of at most 0.00013.
Values sent between devices are 32-bit elements; how exact they have to be, the bound alone decides.
A program may use at most 128 MiB of HBM per device.

```python
import jax
import jax.numpy as jnp
from jax import lax

NV = 512
NC = 2048
NP = 8192
BATCH = 1
ITERS = 2


def block_levels(own_key, dims, pieces, low, top_value):
    def one(axis_at, parts):
        heights = jax.random.uniform(jax.random.fold_in(jax.random.fold_in(own_key, 6), axis_at), (parts,), jnp.float32, low / len(pieces), top_value / len(pieces))
        return jnp.repeat(jnp.exp(heights), dims[axis_at] // parts).reshape((-1,) + (1,) * (len(dims) - axis_at - 1))

    level = one(*pieces[0])
    for cut in pieces[1:]:
        level = level * one(*cut)
    return level


def scatter_about(stream_key, dims, spread, bound, cuts=(), dtype=jnp.bfloat16):
    loudness = block_levels(stream_key, dims, cuts, -0.22, 0.18) if cuts else 1.0
    array = jax.random.normal(stream_key, dims, jnp.float32) * spread * loudness
    return jnp.minimum(jnp.maximum(array, -bound), bound).astype(dtype)


def setup_inputs(seed: int = 0) -> dict:
    key_list = jax.random.split(jax.random.key(seed), 7)
    vectors = scatter_about(key_list[0], (BATCH, NV, NC), 1.0, 6.0, ((1, 4), (2, 8)), jnp.float32)
    eval_energy = jnp.clip(-2.0 + 1.8 * jax.random.uniform(key_list[1], (NV,), jnp.float32) ** block_levels(key_list[1], (NV,), ((0, 4),), -0.2, 0.2), -2.0, -0.2)
    cond_energy = jnp.clip(0.2 + 1.8 * jax.random.uniform(key_list[2], (NC,), jnp.float32) ** block_levels(key_list[2], (NC,), ((0, 8),), -0.2, 0.2), 0.2, 2.0)
    val_orbitals = scatter_about(key_list[3], (NV, NP), NV ** -0.5, 0.25, ((0, 8), (1, 4)), jnp.float32)
    cond_orbitals = scatter_about(key_list[4], (NC, NP), NC ** -0.5, 0.125, ((0, 4), (1, 8)), jnp.float32)
    screened = scatter_about(key_list[5], (NP, NP), (NP * NP // (4 * NV * NC)) ** -0.5, 1.5, ((0, 4), (1, 8)), jnp.float32)
    return dict(vectors=vectors, eval_energy=eval_energy, cond_energy=cond_energy, val_orbitals=val_orbitals, cond_orbitals=cond_orbitals, screened=screened)


CENTER = 2.2
HALF_WIDTH = 2.0


def apply_direct(vec, val_orbitals, cond_orbitals, screened):
    highest = lax.Precision.HIGHEST

    def single(x):
        pair = jnp.dot(x, cond_orbitals, precision=highest, preferred_element_type=jnp.float32)
        mixed = jnp.dot(val_orbitals.T, pair, precision=highest, preferred_element_type=jnp.float32)
        weighted = mixed * screened
        back = jnp.dot(val_orbitals, weighted, precision=highest, preferred_element_type=jnp.float32)
        return jnp.dot(back, cond_orbitals.T, precision=highest, preferred_element_type=jnp.float32)

    return lax.map(single, vec)


def reference(vectors, eval_energy, cond_energy, val_orbitals, cond_orbitals, screened):
    ediff = cond_energy[None, None, :] - eval_energy[None, :, None]
    older = vectors
    newer = vectors
    for step in range(ITERS):
        hamil = ediff * newer - apply_direct(newer, val_orbitals, cond_orbitals, screened)
        scaled = (hamil - CENTER * newer) / HALF_WIDTH
        if step == 0:
            following = scaled
        else:
            following = 2.0 * scaled - older
        older = newer
        newer = following
    return newer
```

```python
import functools

import jax
import jax.numpy as jnp
from jax import lax
from jax.experimental import pallas as pl
from jax.experimental.pallas import tpu as pltpu
from jax.sharding import PartitionSpec as P

ITERS = 2
PIECES = 32
PIECES_AHEAD = 6

CENTER = 2.2
HALF_WIDTH = 2.0


def dot(dims, a, b):
    return lax.dot_general(
        a, b, (dims, ((), ())), precision=lax.Precision.HIGH, preferred_element_type=jnp.float32
    )


def line_kernel(axis, count, part_ref, out_ref, came, last, came_send, came_recv, last_send, last_recv):
    at = lax.axis_index(axis)
    half = count // 2
    left = at < half
    inner = jnp.where(left, at + 1, at - 1)
    outer = jnp.where(left, at - 1, at + 1)
    edge = (at == 0) | (at == count - 1)
    middle = (at == half - 1) | (at == half)
    pieces = part_ref.shape[0]

    def copy(source, target, send, recv, to):
        return pltpu.make_async_remote_copy(
            src_ref=source, dst_ref=target, send_sem=send, recv_sem=recv,
            device_id={axis: to}, device_id_type=pl.DeviceIdType.MESH,
        )

    def to_inner(t):
        return copy(out_ref.at[t], came.at[t], came_send.at[t], came_recv.at[t], inner)

    def across(t):
        return copy(out_ref.at[t], last.at[t], came_send.at[t], last_recv.at[t], inner)

    def to_outer(t):
        return copy(last.at[t], last.at[t], last_send.at[t], last_recv.at[t], outer)

    barrier = pltpu.get_barrier_semaphore()
    pl.semaphore_signal(barrier, inc=1, device_id={axis: inner}, device_id_type=pl.DeviceIdType.MESH)

    @pl.when(jnp.logical_not(edge))
    def _():
        pl.semaphore_signal(
            barrier, inc=1, device_id={axis: outer}, device_id_type=pl.DeviceIdType.MESH
        )
        pl.semaphore_wait(barrier, 2)

    @pl.when(edge)
    def _():
        pl.semaphore_wait(barrier, 1)

    def inward(t, carry):
        out_ref[t] = part_ref[t]

        @pl.when(jnp.logical_not(edge))
        def _():
            to_inner(t).wait_recv()
            out_ref[t] = part_ref[t] + came[t]

        @pl.when(middle)
        def _():
            across(t).start()

        @pl.when(jnp.logical_not(middle))
        def _():
            to_inner(t).start()

        return carry

    def outward(t, carry):
        across(t).wait_recv()

        @pl.when(middle)
        def _():
            last[t] = last[t] + out_ref[t]

        @pl.when(jnp.logical_not(edge))
        def _():
            to_outer(t).start()

        to_inner(t).wait_send()
        out_ref[t] = last[t]
        return carry

    def drain(t, carry):
        @pl.when(jnp.logical_not(edge))
        def _():
            to_outer(t).wait_send()

        return carry

    @pl.when(edge)
    def _():
        lax.fori_loop(0, pieces, inward, 0)
        lax.fori_loop(0, pieces, outward, 0)

    @pl.when(jnp.logical_not(edge))
    def _():
        def both(t, carry):
            inward(t, carry)
            return outward(t - PIECES_AHEAD, carry)

        lax.fori_loop(0, PIECES_AHEAD, inward, 0)
        lax.fori_loop(PIECES_AHEAD, pieces, both, 0)
        lax.fori_loop(pieces - PIECES_AHEAD, pieces, outward, 0)

    lax.fori_loop(0, pieces, drain, 0)


def line_sum(part, axis, count):
    if count == 1:
        return part
    if count % 2:
        return lax.psum(part, axis)
    rows, columns = part.shape
    cut = (PIECES, rows // PIECES, columns)
    total = pl.pallas_call(
        functools.partial(line_kernel, axis, count),
        out_shape=jax.ShapeDtypeStruct(cut, jnp.float32),
        in_specs=[pl.BlockSpec(memory_space=pltpu.VMEM)],
        out_specs=pl.BlockSpec(memory_space=pltpu.VMEM),
        scratch_shapes=[pltpu.VMEM(cut, jnp.float32)] * 2 + [pltpu.SemaphoreType.DMA((PIECES,))] * 4,
        compiler_params=pltpu.CompilerParams(collective_id=0, has_side_effects=True),
    )(part.reshape(cut))
    return total.reshape(part.shape)


def cube_sum(part, axis, count, order):
    at = lax.axis_index(axis)
    for bit in order:
        pairs = [(i, i ^ (1 << bit)) for i in range(count)]
        mine = (at >> bit) & 1
        rows = part.shape[0] // 2
        gone = lax.dynamic_slice_in_dim(part, (1 - mine) * rows, rows, 0)
        kept = lax.dynamic_slice_in_dim(part, mine * rows, rows, 0)
        part = kept + lax.ppermute(gone, axis, pairs)
    for bit in reversed(order):
        pairs = [(i, i ^ (1 << bit)) for i in range(count)]
        mine = (at >> bit) & 1
        got = lax.ppermute(part, axis, pairs)
        part = jnp.where(
            mine == 0, jnp.concatenate([part, got], 0), jnp.concatenate([got, part], 0)
        )
    return part


def plane_sum(part, axis, count):
    if count & (count - 1):
        return lax.psum(part, axis)
    bits = list(range(count.bit_length() - 1))
    other = bits[:1] + bits[1:][::-1]
    mid = part.shape[0] // 2
    return jnp.concatenate(
        [cube_sum(part[:mid], axis, count, bits), cube_sum(part[mid:], axis, count, other)], 0
    )


def per_device(
    n_pts, n_val, vectors, eval_energy, cond_energy, val_orbitals, cond_orbitals, screened
):
    bands, width = vectors.shape[1], vectors.shape[2]
    own = cond_orbitals.shape[0]
    per = own // width
    j, p = lax.axis_index("val"), lax.axis_index("pts")
    mine = (p // per) == j
    place = (p % per) * width

    val_whole = lax.all_gather(val_orbitals, "pts", axis=0, tiled=True)

    extra = jnp.stack([cond_energy, jnp.pad(eval_energy, (0, width - bands))])
    extra = jnp.pad(extra, ((0, 6), (0, 0)))
    held = lax.all_gather(jnp.concatenate([vectors[0], extra]), "val", axis=0)
    eval_whole = held[:, bands + 1, :bands].reshape(-1)
    rows = held[:, :bands].reshape(-1, width)
    valence = rows.shape[0]
    rows = jnp.concatenate([rows, jnp.pad(cond_energy[None], ((0, 16 * n_pts - 1), (0, 0)))])
    spread = lax.dynamic_update_slice(
        jnp.zeros((rows.shape[0], own), jnp.float32),
        jnp.where(mine, rows, 0.0),
        (jnp.zeros_like(place), place),
    )
    spread = plane_sum(spread, "pts", n_pts)
    older = newer = spread[:valence]
    ediff = spread[valence][None, :] - eval_whole[:, None]

    for step in range(ITERS):
        pair = line_sum(dot(((1,), (0,)), newer, cond_orbitals), "val", n_val)
        weighted = dot(((0,), (0,)), val_whole, pair) * screened
        back = line_sum(dot(((1,), (0,)), val_whole, weighted), "val", n_val)
        direct = dot(((1,), (1,)), back, cond_orbitals)
        direct = plane_sum(direct, "pts", n_pts)
        hamil = ediff * newer - direct
        scaled = (hamil - CENTER * newer) / HALF_WIDTH
        if step == 0:
            following = scaled
        else:
            following = 2.0 * scaled - older
        older = newer
        newer = following

    out = lax.dynamic_slice_in_dim(newer, place, width, 1)
    out = lax.psum_scatter(jnp.where(mine, out, 0.0), "val", scatter_dimension=0, tiled=True)
    return out[None]


def solution(mesh):
    placed = (
        P(None, "val", "pts"),
        P("val"),
        P("pts"),
        P("pts", "val"),
        P("val", "pts"),
        P("val", "pts"),
    )
    n_pts, n_val = mesh.shape["pts"], mesh.shape["val"]

    def body(*args):
        return per_device(n_pts, n_val, *args)

    return jax.shard_map(
        body, mesh=mesh, in_specs=placed, out_specs=P(None, "val", "pts"), check_vma=False
    )
```
